32 devices in a mesh: rows: 8 (over z, x), cols: 4 (over y, core).
Axes of the slice: x: 2, y: 2, z: 4, core: 2. Of those that a mesh axis runs over, the one named last changes fastest.
Arguments:
- panel_t: float32 [16, 2048], P(None, ('rows', 'cols')), may hold values from -6 to 6
- kinship: float32 [2048, 2048], P('rows', 'cols'), may hold values from -0.125 to 0.125
Outputs:
- kin_panel_t: float32 [16, 2048], P(None, ('rows', 'cols'))
- score: float32 [16, 16], replicated
The draws below stay inside these ranges and needn't reach their ends.
All inputs are finite; a program needn't handle non-finite values.
Results may differ from the reference program's by a relative error of at most 0.00008.
Values sent between devices are 32-bit elements; how exact they have to be, the bound alone decides.
A program may use at most 64 MiB of HBM per device.

```python
import jax
import jax.numpy as jnp
from jax import lax

TRAITS = 16
SAMPLES = 2048


def block_levels(rng, shape, pieces, smallest, largest):
    loudness, own = 1.0, jax.random.fold_in(rng, 6)
    for dim, parts in pieces:
        heights = jnp.exp(jax.random.uniform(jax.random.fold_in(own, dim), (parts,), jnp.float32, smallest / len(pieces), largest / len(pieces)))
        loudness = loudness * jnp.repeat(heights, shape[dim] // parts).reshape([-1 if axis == dim else 1 for axis in range(len(shape))])
    return loudness


def centred(key, shape, scale, most, pieces=(), dtype=jnp.bfloat16):
    factor_of = block_levels(key, shape, pieces, -0.22, 0.18) if pieces else 1.0
    drawn = jax.random.normal(key, shape, jnp.float32) * scale * factor_of
    return jnp.minimum(jnp.maximum(drawn, -most), most).astype(dtype)


def setup_inputs(seed: int = 0) -> dict:
    streams_of = jax.random.split(jax.random.key(seed), 3)
    panel_t = centred(streams_of[0], (TRAITS, SAMPLES), 1.0, 6.0, ((1, 32),), jnp.float32)
    kinship = centred(streams_of[1], (SAMPLES, SAMPLES), SAMPLES ** -0.5, 0.125, ((0, 8), (1, 4)), jnp.float32)
    return dict(panel_t=panel_t, kinship=kinship)


def reference(panel_t, kinship):
    kin_panel_t = lax.dot_general(panel_t, kinship, (((1,), (1,)), ((), ())), precision=lax.Precision.HIGHEST, preferred_element_type=jnp.float32)
    score = lax.dot_general(panel_t, kin_panel_t, (((1,), (1,)), ((), ())), precision=lax.Precision.HIGHEST, preferred_element_type=jnp.float32)
    score = score / jnp.sqrt(jnp.float32(panel_t.shape[1]))
    return (kin_panel_t, score)
```

```python
import functools
import math

import jax
import jax.numpy as jnp
from jax import lax
from jax.experimental import pallas as pl
from jax.experimental.pallas import tpu as pltpu
from jax.sharding import PartitionSpec as P

MESH = pl.DeviceIdType.MESH
LANES = 128
SUBLANES = 8


def dot(left, right, contract):
    return lax.dot_general(
        left,
        right,
        (contract, ((), ())),
        precision=lax.Precision.HIGHEST,
        preferred_element_type=jnp.float32,
    )


def group_mask(traits):
    row = lax.broadcasted_iota(jnp.int32, (traits, LANES), 0)
    lane = lax.broadcasted_iota(jnp.int32, (traits, LANES), 1)
    return (row % SUBLANES) == (lane // traits)


def kernel(
    rows,
    cols,
    panel_hbm,
    kin_hbm,
    out_ref,
    score_ref,
    panel,
    kin,
    zbuf,
    slab,
    block,
    part,
    landed,
    form,
    plane_forms,
    line_form,
    line_forms,
    local_sem,
    z_send,
    z_recv,
    slab_send,
    slab_recv,
    block_send,
    block_recv,
    part_send,
    part_recv,
    plane_send,
    plane_recv,
    line_send,
    line_recv,
):
    depth = rows // cols
    plane = depth * cols
    traits, own = panel.shape
    row, col = lax.axis_index("rows"), lax.axis_index("cols")
    zz, xx = row // depth, row % depth
    mine = xx * cols + col

    def z_mate(k):
        return (k * depth + xx, col)

    def plane_mate(m):
        return (zz * depth + m // cols, m % cols)

    get_panel = pltpu.make_async_copy(panel_hbm, panel, local_sem.at[0])
    get_panel.start()
    get_kin = pltpu.make_async_copy(kin_hbm, kin, local_sem.at[1])
    get_kin.start()

    barrier = pltpu.get_barrier_semaphore()
    for step in range(1, cols):
        pl.semaphore_signal(
            barrier, inc=1, device_id=z_mate((zz + step) % cols), device_id_type=MESH
        )
    for step in range(1, plane):
        pl.semaphore_signal(
            barrier, inc=1, device_id=plane_mate((mine + step) % plane), device_id_type=MESH
        )
    get_panel.wait()
    keep_line = pltpu.make_async_copy(panel, zbuf.at[zz], z_recv.at[zz])
    keep_line.start()
    keep_slab = pltpu.make_async_copy(panel, slab.at[col], slab_recv.at[col])
    keep_slab.start()
    pl.semaphore_wait(barrier, cols - 1 + plane - 1)

    def remote(src, dst, send, recv, where):
        return pltpu.make_async_remote_copy(
            src_ref=src,
            dst_ref=dst,
            send_sem=send,
            recv_sem=recv,
            device_id=where,
            device_id_type=MESH,
        )

    sends = []
    for step in range(1, cols):
        k = (zz + step) % cols
        copy = remote(panel, zbuf.at[zz], z_send.at[step], z_recv.at[zz], z_mate(k))
        copy.start()
        sends.append(copy)
    for step in range(1, cols):
        c = (col + step) % cols
        copy = remote(panel, slab.at[col], slab_send.at[step], slab_recv.at[col], (row, c))
        copy.start()
        sends.append(copy)

    def arrived(buf, sem, slot):
        remote(buf.at[slot], buf.at[slot], sem.at[slot], sem.at[slot], (row, col)).wait_recv()

    keep_slab.wait()
    for step in range(1, cols):
        arrived(slab, slab_recv, (col + step) % cols)
    get_kin.wait()
    slab_panel = jnp.concatenate([slab[c] for c in range(cols)], axis=1)
    side = dot(slab_panel, kin[...], ((1,), (0,)))

    keep_line.wait()
    for step in range(1, cols):
        arrived(zbuf, z_recv, (zz + step) % cols)
    keep_block = pltpu.make_async_copy(zbuf.at[col], block.at[mine], block_recv.at[mine])
    keep_block.start()
    for step in range(1, plane):
        m = (mine + step) % plane
        copy = remote(
            zbuf.at[m % cols], block.at[mine], block_send.at[step], block_recv.at[mine], plane_mate(m)
        )
        copy.start()
        sends.append(copy)
    keep_block.wait()
    for step in range(1, plane):
        arrived(block, block_recv, (mine + step) % plane)

    block_panel = jnp.concatenate([block[m] for m in range(plane)], axis=1)
    wide = jnp.concatenate([block_panel] * (LANES // traits), axis=0)
    spread = dot(side, wide, ((1,), (1,)))
    mask = group_mask(traits)
    spread = jnp.where(mask, spread, 0.0)
    form[...] = jnp.sum(spread.reshape(traits // SUBLANES, SUBLANES, LANES), axis=1)
    for step in range(1, plane):
        m = (mine + step) % plane
        copy = remote(
            form, plane_forms.at[mine], plane_send.at[step], plane_recv.at[mine], plane_mate(m)
        )
        copy.start()
        sends.append(copy)
    plane_forms[mine] = form[...]

    value = dot(block_panel, kin[...], ((1,), (1,)))
    for c in range(cols):
        part[c] = value[:, c * own : (c + 1) * own]
    for step in range(1, cols):
        c = (col + step) % cols
        copy = remote(part.at[c], landed.at[col], part_send.at[step], part_recv.at[col], (row, c))
        copy.start()
        sends.append(copy)
    landed[col] = part[col]

    for step in range(1, plane):
        arrived(plane_forms, plane_recv, (mine + step) % plane)
    total = plane_forms[0]
    for m in range(1, plane):
        total += plane_forms[m]
    line_form[...] = total
    for step in range(1, cols):
        k = (zz + step) % cols
        copy = remote(
            line_form, line_forms.at[zz], line_send.at[step], line_recv.at[zz], z_mate(k)
        )
        copy.start()
        sends.append(copy)
    line_forms[zz] = total

    for step in range(1, cols):
        arrived(landed, part_recv, (col + step) % cols)
    result = landed[0]
    for c in range(1, cols):
        result += landed[c]
    out_ref[...] = result

    for step in range(1, cols):
        arrived(line_forms, line_recv, (zz + step) % cols)
    total = line_forms[0]
    for k in range(1, cols):
        total += line_forms[k]
    spread = jnp.concatenate(
        [
            jnp.broadcast_to(total[i : i + 1, :], (SUBLANES, LANES))
            for i in range(traits // SUBLANES)
        ],
        axis=0,
    )
    spread = jnp.where(mask, spread, 0.0)
    shift = LANES // 2
    while shift >= traits:
        spread += pltpu.roll(spread, shift, 1)
        shift //= 2
    score_ref[...] = spread[:, :traits] / math.sqrt(rows * cols * own)
    for copy in sends:
        copy.wait_send()


def shards(rows, cols, panel_t, kinship):
    traits, own = panel_t.shape
    plane = rows // cols * cols
    vmem = pltpu.VMEM
    dma = pltpu.SemaphoreType.DMA
    form = (traits * traits // LANES, LANES)
    f32 = jnp.float32
    return tuple(
        pl.pallas_call(
            functools.partial(kernel, rows, cols),
            out_shape=(
                jax.ShapeDtypeStruct((traits, own), f32),
                jax.ShapeDtypeStruct((traits, traits), f32),
            ),
            in_specs=[pl.BlockSpec(memory_space=pl.ANY)] * 2,
            out_specs=(pl.BlockSpec(memory_space=vmem),) * 2,
            scratch_shapes=[
                vmem((traits, own), f32),
                vmem(kinship.shape, f32),
                vmem((cols, traits, own), f32),
                vmem((cols, traits, own), f32),
                vmem((plane, traits, own), f32),
                vmem((cols, traits, own), f32),
                vmem((cols, traits, own), f32),
                vmem(form, f32),
                vmem((plane,) + form, f32),
                vmem(form, f32),
                vmem((cols,) + form, f32),
                dma((2,)),
                dma((cols,)),
                dma((cols,)),
                dma((cols,)),
                dma((cols,)),
                dma((plane,)),
                dma((plane,)),
                dma((cols,)),
                dma((cols,)),
                dma((plane,)),
                dma((plane,)),
                dma((cols,)),
                dma((cols,)),
            ],
            compiler_params=pltpu.CompilerParams(collective_id=0, has_side_effects=True),
        )(panel_t, kinship)
    )


def solution(mesh):
    rows, cols = mesh.shape["rows"], mesh.shape["cols"]
    return jax.shard_map(
        functools.partial(shards, rows, cols),
        mesh=mesh,
        in_specs=(P(None, ("rows", "cols")), P("rows", "cols")),
        out_specs=(P(None, ("rows", "cols")), P()),
        check_vma=False,
    )
```

```python
import functools
import math

import jax
import jax.numpy as jnp
from jax import lax
from jax.experimental import pallas as pl
from jax.experimental.pallas import tpu as pltpu
from jax.sharding import PartitionSpec as P

MESH = pl.DeviceIdType.MESH
LANES = 128
SUBLANES = 8


def split(x):
    high = x.astype(jnp.bfloat16)
    rest = x - high.astype(jnp.float32)
    mid = rest.astype(jnp.bfloat16)
    low = (rest - mid.astype(jnp.float32)).astype(jnp.bfloat16)
    return high, mid, low


def dot(left, right, dims):
    n = left[0].shape[0]

    def one(pieces, weights):
        return lax.dot_general(
            jnp.concatenate(pieces, axis=0),
            weights,
            (dims, ((), ())),
            preferred_element_type=jnp.float32,
        )

    high, mid, low = one(left, right[0]), one(left[:2], right[1]), one(left[:1], right[2])
    small = high[2 * n :] + mid[n:] + low
    return high[:n] + (high[n : 2 * n] + mid[:n] + small)


def remote(src, dst, send, recv, where):
    return pltpu.make_async_remote_copy(
        src_ref=src,
        dst_ref=dst,
        send_sem=send,
        recv_sem=recv,
        device_id=where,
        device_id_type=MESH,
    )


def kernel(
    rows,
    cols,
    panel_hbm,
    kin_hbm,
    out_ref,
    score_ref,
    panel,
    kin,
    kin_high,
    kin_mid,
    kin_low,
    slab,
    block,
    part,
    landed,
    forms,
    panel_sem,
    kin_sem,
    slab_send,
    slab_recv,
    block_send,
    block_recv,
    part_send,
    part_recv,
    forms_send,
    forms_recv,
):
    count = rows * cols
    depth = rows // cols
    plane = depth * cols
    traits, own = panel.shape
    row, col = lax.axis_index("rows"), lax.axis_index("cols")
    me = row * cols + col
    zz = row // depth
    mine = me % plane

    def others(body):
        back = jnp.where(zz < cols // 2, 1, 0)
        base = me + back * count
        sign = 1 - 2 * back

        def step_of(step, carry):
            other = (base + sign * step) % count
            body((other // cols, other % cols), step)
            return carry

        lax.fori_loop(1, count, step_of, 0)

    get_panel = pltpu.make_async_copy(panel_hbm, panel, panel_sem)
    get_panel.start()
    get_kin = pltpu.make_async_copy(kin_hbm, kin, kin_sem)
    get_kin.start()

    barrier = pltpu.get_barrier_semaphore()
    others(
        lambda where, step: pl.semaphore_signal(
            barrier, inc=1, device_id=where, device_id_type=MESH
        )
    )
    get_panel.wait()
    slab[col] = panel[...]
    get_kin.wait()
    kin_high[...], kin_mid[...], kin_low[...] = split(kin[...])
    pl.semaphore_wait(barrier, count - 1)

    keep_block = pltpu.make_async_copy(panel, block.at[mine], block_recv)
    send_block = remote(panel, block.at[mine], block_send, block_recv, (row, zz))
    for step in range(1, rows):
        r = (row + step) % rows
        remote(panel, block.at[mine], block_send, block_recv, (r, zz)).start()

    @pl.when(col == zz)
    def _():
        keep_block.start()

    @pl.when(col != zz)
    def _():
        send_block.start()

    for step in range(1, cols):
        c = (col + step) % cols
        remote(panel, slab.at[col], slab_send, slab_recv, (row, c)).start()

    def wait_bytes(ref, sem):
        pltpu.make_async_copy(ref, ref, sem).wait()

    wait_bytes(slab.at[pl.ds(0, cols - 1)], slab_recv)
    weights = (kin_high[...], kin_mid[...], kin_low[...])
    slab_panel = jnp.concatenate([slab[c] for c in range(cols)], axis=1)
    side = dot(split(slab_panel / math.sqrt(count * own)), weights, ((1,), (0,)))
    wide = tuple(jnp.concatenate([x] * (LANES // traits), axis=0) for x in split(side))

    wait_bytes(block, block_recv)
    block_panel = split(jnp.concatenate([block[m] for m in range(plane)], axis=1))
    spread = dot(block_panel, wide, ((1,), (1,)))
    sublane = lax.broadcasted_iota(jnp.int32, (traits, LANES), 0) % SUBLANES
    group = lax.broadcasted_iota(jnp.int32, (traits, LANES), 1) // traits
    spread = jnp.where(sublane == group, spread, 0.0)
    forms[me] = jnp.sum(spread.reshape(traits // SUBLANES, SUBLANES, LANES), axis=1)
    others(
        lambda where, step: remote(
            forms.at[me], forms.at[me], forms_send, forms_recv, where
        ).start()
    )

    value = dot(block_panel, (kin_high[...], kin_mid[...], kin_low[...]), ((1,), (1,)))
    for c in range(cols):
        part[c] = value[:, c * own : (c + 1) * own]
    for step in range(1, cols):
        c = (col + step) % cols
        remote(part.at[c], landed.at[col], part_send, part_recv, (row, c)).start()
    landed[col] = part[col]

    wait_bytes(landed.at[pl.ds(0, cols - 1)], part_recv)
    result = landed[0]
    for c in range(1, cols):
        result += landed[c]
    out_ref[...] = result

    wait_bytes(block.at[pl.ds(0, rows - 1)], block_send)

    @pl.when(col != zz)
    def _():
        send_block.wait_send()

    wait_bytes(slab.at[pl.ds(0, cols - 1)], slab_send)
    wait_bytes(landed.at[pl.ds(0, cols - 1)], part_send)
    wait_bytes(forms.at[pl.ds(0, count - 1)], forms_send)
    wait_bytes(forms.at[pl.ds(0, count - 1)], forms_recv)
    total = jnp.sum(forms[...], axis=0)
    spread = jnp.concatenate(
        [
            jnp.broadcast_to(total[i : i + 1, :], (SUBLANES, LANES))
            for i in range(traits // SUBLANES)
        ],
        axis=0,
    )
    spread = jnp.where(sublane == group, spread, 0.0)
    score_ref[...] = jnp.sum(spread.T.reshape(LANES // traits, traits, traits), axis=0)


def shards(rows, cols, panel_t, kinship):
    traits, own = panel_t.shape
    plane = rows // cols * cols
    vmem = pltpu.VMEM
    dma = pltpu.SemaphoreType.DMA
    f32, bf16 = jnp.float32, jnp.bfloat16
    chunk = (traits, own)
    return tuple(
        pl.pallas_call(
            functools.partial(kernel, rows, cols),
            out_shape=(vmem(chunk, f32), vmem((traits, traits), f32)),
            in_specs=[pl.BlockSpec(memory_space=pl.ANY)] * 2,
            out_specs=(pl.BlockSpec(memory_space=vmem),) * 2,
            scratch_shapes=[
                vmem(chunk, f32),
                vmem(kinship.shape, f32),
                vmem(kinship.shape, bf16),
                vmem(kinship.shape, bf16),
                vmem(kinship.shape, bf16),
                vmem((cols,) + chunk, f32),
                vmem((plane,) + chunk, f32),
                vmem((cols,) + chunk, f32),
                vmem((cols,) + chunk, f32),
                vmem((rows * cols, traits * traits // LANES, LANES), f32),
            ]
            + [dma(())] * 10,
            compiler_params=pltpu.CompilerParams(collective_id=0, has_side_effects=True),
        )(panel_t, kinship)
    )


def solution(mesh):
    rows, cols = mesh.shape["rows"], mesh.shape["cols"]
    return jax.shard_map(
        functools.partial(shards, rows, cols),
        mesh=mesh,
        in_specs=(P(None, ("rows", "cols")), P("rows", "cols")),
        out_specs=(P(None, ("rows", "cols")), P()),
        check_vma=False,
    )
```

```python
import functools
import math

import jax
import jax.numpy as jnp
from jax import lax
from jax.experimental import pallas as pl
from jax.experimental.pallas import tpu as pltpu
from jax.sharding import PartitionSpec as P

MESH = pl.DeviceIdType.MESH
LANES = 128
SUBLANES = 8


def split(x):
    high = x.astype(jnp.bfloat16)
    rest = x - high.astype(jnp.float32)
    mid = rest.astype(jnp.bfloat16)
    low = (rest - mid.astype(jnp.float32)).astype(jnp.bfloat16)
    return high, mid, low


def dot(left, right, dims):
    n = left[0].shape[0]

    def one(pieces, weights):
        return lax.dot_general(
            jnp.concatenate(pieces, axis=0),
            weights,
            (dims, ((), ())),
            preferred_element_type=jnp.float32,
        )

    high, mid, low = one(left, right[0]), one(left[:2], right[1]), one(left[:1], right[2])
    small = high[2 * n :] + mid[n:] + low
    return high[:n] + (high[n : 2 * n] + mid[:n] + small)


def fold(x):
    half = x.shape[0] // 2
    return jnp.concatenate([x[:half], x[half:]], axis=1)


def unfold(x):
    own = x.shape[1] // 2
    return jnp.concatenate([x[:, :own], x[:, own:]], axis=0)


def join(chunks):
    own = chunks[0].shape[1] // 2
    return jnp.concatenate(
        [
            jnp.concatenate([x[:, :own] for x in chunks], axis=1),
            jnp.concatenate([x[:, own:] for x in chunks], axis=1),
        ],
        axis=0,
    )


def remote(src, dst, send, recv, where):
    return pltpu.make_async_remote_copy(
        src_ref=src,
        dst_ref=dst,
        send_sem=send,
        recv_sem=recv,
        device_id=where,
        device_id_type=MESH,
    )


def kernel(
    rows,
    cols,
    panel_hbm,
    kin_hbm,
    out_ref,
    score_ref,
    loaded,
    panel,
    kin,
    kin_high,
    kin_mid,
    kin_low,
    slab,
    block,
    part,
    landed,
    forms,
    panel_sem,
    kin_sem,
    slab_send,
    slab_recv,
    block_send,
    block_recv,
    part_send,
    part_recv,
    forms_send,
    forms_recv,
):
    count = rows * cols
    depth = rows // cols
    plane = depth * cols
    traits, own = panel_hbm.shape
    row, col = lax.axis_index("rows"), lax.axis_index("cols")
    me = row * cols + col
    zz = row // depth
    mine = me % plane

    def others(body):
        back = zz < cols // 2
        peers = [(col + step) % cols for step in range(cols)]

        def row_of(step, carry):
            r = jnp.where(back, row - step, row + step)
            r = jnp.where(r < 0, r + rows, jnp.where(r >= rows, r - rows, r))
            for c in peers:
                body((r, c))
            return carry

        lax.fori_loop(1, rows, row_of, 0)
        for c in peers[1:]:
            body((row, c))

    barrier = pltpu.get_barrier_semaphore()
    others(
        lambda where: pl.semaphore_signal(
            barrier, inc=1, device_id=where, device_id_type=MESH
        )
    )
    get_panel = pltpu.make_async_copy(panel_hbm, loaded, panel_sem)
    get_panel.start()
    get_kin = pltpu.make_async_copy(kin_hbm, kin, kin_sem)
    get_kin.start()
    get_panel.wait()
    panel[...] = fold(loaded[...])
    slab[col] = panel[...]
    pl.semaphore_wait(barrier, count - 1)

    keep_block = pltpu.make_async_copy(panel, block.at[mine], block_recv)
    send_block = remote(panel, block.at[mine], block_send, block_recv, (row, zz))
    for step in range(1, rows):
        r = (row + step) % rows
        remote(panel, block.at[mine], block_send, block_recv, (r, zz)).start()

    @pl.when(col == zz)
    def _():
        keep_block.start()

    @pl.when(col != zz)
    def _():
        send_block.start()

    for step in range(1, cols):
        c = (col + step) % cols
        remote(panel, slab.at[col], slab_send, slab_recv, (row, c)).start()

    def wait_bytes(ref, sem):
        pltpu.make_async_copy(ref, ref, sem).wait()

    get_kin.wait()
    kin_high[...], kin_mid[...], kin_low[...] = split(kin[...])
    wait_bytes(slab.at[pl.ds(0, cols - 1)], slab_recv)
    weights = (kin_high[...], kin_mid[...], kin_low[...])
    slab_panel = join([slab[c] for c in range(cols)])
    side = dot(split(slab_panel / math.sqrt(count * own)), weights, ((1,), (0,)))
    wide = tuple(jnp.concatenate([x] * (LANES // traits), axis=0) for x in split(side))

    wait_bytes(block, block_recv)
    block_panel = split(join([block[m] for m in range(plane)]))
    spread = dot(block_panel, wide, ((1,), (1,)))
    sublane = lax.broadcasted_iota(jnp.int32, (traits, LANES), 0) % SUBLANES
    group = lax.broadcasted_iota(jnp.int32, (traits, LANES), 1) // traits
    spread = jnp.where(sublane == group, spread, 0.0)
    forms[me] = jnp.sum(spread.reshape(traits // SUBLANES, SUBLANES, LANES), axis=1)
    others(
        lambda where: remote(
            forms.at[me], forms.at[me], forms_send, forms_recv, where
        ).start()
    )

    value = dot(block_panel, (kin_high[...], kin_mid[...], kin_low[...]), ((1,), (1,)))
    for c in range(cols):
        part[c] = fold(value[:, c * own : (c + 1) * own])
    for step in range(1, cols):
        c = (col + step) % cols
        remote(part.at[c], landed.at[col], part_send, part_recv, (row, c)).start()
    landed[col] = part[col]

    wait_bytes(landed.at[pl.ds(0, cols - 1)], part_recv)
    result = landed[0]
    for c in range(1, cols):
        result += landed[c]
    out_ref[...] = unfold(result)

    wait_bytes(block.at[pl.ds(0, rows - 1)], block_send)

    @pl.when(col != zz)
    def _():
        send_block.wait_send()

    wait_bytes(slab.at[pl.ds(0, cols - 1)], slab_send)
    wait_bytes(landed.at[pl.ds(0, cols - 1)], part_send)
    wait_bytes(forms.at[pl.ds(0, count - 1)], forms_send)
    wait_bytes(forms.at[pl.ds(0, count - 1)], forms_recv)
    total = jnp.sum(forms[...], axis=0)
    spread = jnp.concatenate(
        [
            jnp.broadcast_to(total[i : i + 1, :], (SUBLANES, LANES))
            for i in range(traits // SUBLANES)
        ],
        axis=0,
    )
    spread = jnp.where(sublane == group, spread, 0.0)
    score_ref[...] = jnp.sum(spread.T.reshape(LANES // traits, traits, traits), axis=0)


def finish(value_ref, form_ref, out_ref, score_ref, sems):
    first = pltpu.make_async_copy(value_ref, out_ref, sems.at[0])
    second = pltpu.make_async_copy(form_ref, score_ref, sems.at[1])
    first.start()
    second.start()
    first.wait()
    second.wait()


def shards(rows, cols, panel_t, kinship):
    traits, own = panel_t.shape
    plane = rows // cols * cols
    vmem = pltpu.VMEM
    dma = pltpu.SemaphoreType.DMA
    f32, bf16 = jnp.float32, jnp.bfloat16
    chunk = (traits // 2, 2 * own)
    value, score = (
        pl.pallas_call(
            functools.partial(kernel, rows, cols),
            out_shape=(vmem((traits, own), f32), vmem((traits, traits), f32)),
            in_specs=[pl.BlockSpec(memory_space=pl.ANY)] * 2,
            out_specs=(pl.BlockSpec(memory_space=vmem),) * 2,
            scratch_shapes=[
                vmem((traits, own), f32),
                vmem(chunk, f32),
                vmem(kinship.shape, f32),
                vmem(kinship.shape, bf16),
                vmem(kinship.shape, bf16),
                vmem(kinship.shape, bf16),
                vmem((cols,) + chunk, f32),
                vmem((plane,) + chunk, f32),
                vmem((cols,) + chunk, f32),
                vmem((cols,) + chunk, f32),
                vmem((rows * cols, traits * traits // LANES, LANES), f32),
            ]
            + [dma(())] * 10,
            compiler_params=pltpu.CompilerParams(collective_id=0, has_side_effects=True),
        )(panel_t, kinship)
    )
    return tuple(
        pl.pallas_call(
            finish,
            out_shape=(
                jax.ShapeDtypeStruct((traits, own), f32),
                jax.ShapeDtypeStruct((traits, traits), f32),
            ),
            in_specs=[pl.BlockSpec(memory_space=pl.ANY)] * 2,
            out_specs=(pl.BlockSpec(memory_space=pl.ANY),) * 2,
            scratch_shapes=[dma((2,))],
            compiler_params=pltpu.CompilerParams(vmem_limit_bytes=1024 * 1024),
        )(value, score)
    )


def solution(mesh):
    rows, cols = mesh.shape["rows"], mesh.shape["cols"]
    return jax.shard_map(
        functools.partial(shards, rows, cols),
        mesh=mesh,
        in_specs=(P(None, ("rows", "cols")), P("rows", "cols")),
        out_specs=(P(None, ("rows", "cols")), P()),
        check_vma=False,
    )
```

```python
import functools
import math

import jax
import jax.numpy as jnp
from jax import lax
from jax.experimental import pallas as pl
from jax.experimental.pallas import tpu as pltpu
from jax.sharding import PartitionSpec as P

MESH = pl.DeviceIdType.MESH
LANES = 128
SUBLANES = 8


def split(x):
    high = x.astype(jnp.bfloat16)
    rest = x - high.astype(jnp.float32)
    mid = rest.astype(jnp.bfloat16)
    low = (rest - mid.astype(jnp.float32)).astype(jnp.bfloat16)
    return high, mid, low


def dot(left, right, dims):
    n = left[0].shape[0]

    def one(pieces, weights):
        return lax.dot_general(
            jnp.concatenate(pieces, axis=0),
            weights,
            (dims, ((), ())),
            preferred_element_type=jnp.float32,
        )

    high, mid, low = one(left, right[0]), one(left[:2], right[1]), one(left[:1], right[2])
    small = high[2 * n :] + mid[n:] + low
    return high[:n] + (high[n : 2 * n] + mid[:n] + small)


def fold(x):
    half = x.shape[0] // 2
    return jnp.concatenate([x[:half], x[half:]], axis=1)


def unfold(x):
    own = x.shape[1] // 2
    return jnp.concatenate([x[:, :own], x[:, own:]], axis=0)


def join(chunks):
    own = chunks[0].shape[1] // 2
    return jnp.concatenate(
        [
            jnp.concatenate([x[:, :own] for x in chunks], axis=1),
            jnp.concatenate([x[:, own:] for x in chunks], axis=1),
        ],
        axis=0,
    )


def remote(src, dst, send, recv, where):
    return pltpu.make_async_remote_copy(
        src_ref=src,
        dst_ref=dst,
        send_sem=send,
        recv_sem=recv,
        device_id=where,
        device_id_type=MESH,
    )


def kernel(
    rows,
    cols,
    panel_hbm,
    kin_hbm,
    out_ref,
    score_ref,
    loaded,
    panel,
    kin,
    kin_high,
    kin_mid,
    kin_low,
    slab,
    block,
    part,
    landed,
    forms,
    panel_sem,
    kin_sem,
    slab_send,
    slab_recv,
    block_send,
    block_recv,
    part_send,
    part_recv,
    forms_send,
    forms_recv,
):
    count = rows * cols
    depth = rows // cols
    plane = depth * cols
    traits, own = panel_hbm.shape
    row, col = lax.axis_index("rows"), lax.axis_index("cols")
    me = row * cols + col
    zz = row // depth
    mine = me % plane

    def others(body):
        back = zz < cols // 2
        peers = [(col + step) % cols for step in range(cols)]

        def row_of(step, carry):
            r = jnp.where(back, row - step, row + step)
            r = jnp.where(r < 0, r + rows, jnp.where(r >= rows, r - rows, r))
            for c in peers:
                body((r, c))
            return carry

        lax.fori_loop(1, rows, row_of, 0)
        for c in peers[1:]:
            body((row, c))

    barrier = pltpu.get_barrier_semaphore()
    others(
        lambda where: pl.semaphore_signal(
            barrier, inc=1, device_id=where, device_id_type=MESH
        )
    )
    get_panel = pltpu.make_async_copy(panel_hbm, loaded, panel_sem)
    get_panel.start()
    get_kin = pltpu.make_async_copy(kin_hbm, kin, kin_sem)
    get_kin.start()
    get_panel.wait()
    panel[...] = fold(loaded[...])
    slab[col] = panel[...]
    pl.semaphore_wait(barrier, count - 1)

    for step in range(1, cols):
        c = (col + step) % cols
        remote(panel, slab.at[col], slab_send, slab_recv, (row, c)).start()

    keep_block = pltpu.make_async_copy(panel, block.at[mine], block_recv)
    send_block = remote(panel, block.at[mine], block_send, block_recv, (row, zz))
    sign = jnp.where(zz < cols // 2, rows - 1, 1)
    for step in range(1, rows):
        r = (row + sign * step) % rows
        remote(panel, block.at[mine], block_send, block_recv, (r, zz)).start()

    @pl.when(col == zz)
    def _():
        keep_block.start()

    @pl.when(col != zz)
    def _():
        send_block.start()

    def wait_bytes(ref, sem):
        pltpu.make_async_copy(ref, ref, sem).wait()

    get_kin.wait()
    kin_high[...], kin_mid[...], kin_low[...] = split(kin[...])
    wait_bytes(slab.at[pl.ds(0, cols - 1)], slab_recv)
    weights = (kin_high[...], kin_mid[...], kin_low[...])
    slab_panel = join([slab[c] for c in range(cols)])
    side = dot(split(slab_panel / math.sqrt(count * own)), weights, ((1,), (0,)))
    wide = tuple(jnp.concatenate([x] * (LANES // traits), axis=0) for x in split(side))

    wait_bytes(block, block_recv)
    block_panel = split(join([block[m] for m in range(plane)]))
    spread = dot(block_panel, wide, ((1,), (1,)))
    sublane = lax.broadcasted_iota(jnp.int32, (traits, LANES), 0) % SUBLANES
    group = lax.broadcasted_iota(jnp.int32, (traits, LANES), 1) // traits
    spread = jnp.where(sublane == group, spread, 0.0)
    forms[me] = jnp.sum(spread.reshape(traits // SUBLANES, SUBLANES, LANES), axis=1)
    others(
        lambda where: remote(
            forms.at[me], forms.at[me], forms_send, forms_recv, where
        ).start()
    )

    value = dot(block_panel, (kin_high[...], kin_mid[...], kin_low[...]), ((1,), (1,)))
    for c in range(cols):
        part[c] = fold(value[:, c * own : (c + 1) * own])
    for step in range(1, cols):
        c = (col + step) % cols
        remote(part.at[c], landed.at[col], part_send, part_recv, (row, c)).start()
    landed[col] = part[col]

    wait_bytes(landed.at[pl.ds(0, cols - 1)], part_recv)
    result = landed[0]
    for c in range(1, cols):
        result += landed[c]
    out_ref[...] = unfold(result)

    wait_bytes(block.at[pl.ds(0, rows - 1)], block_send)

    @pl.when(col != zz)
    def _():
        send_block.wait_send()

    wait_bytes(slab.at[pl.ds(0, cols - 1)], slab_send)
    wait_bytes(landed.at[pl.ds(0, cols - 1)], part_send)
    wait_bytes(forms.at[pl.ds(0, count - 1)], forms_send)
    wait_bytes(forms.at[pl.ds(0, count - 1)], forms_recv)
    total = jnp.sum(forms[...], axis=0)
    spread = jnp.concatenate(
        [
            jnp.broadcast_to(total[i : i + 1, :], (SUBLANES, LANES))
            for i in range(traits // SUBLANES)
        ],
        axis=0,
    )
    spread = jnp.where(sublane == group, spread, 0.0)
    score_ref[...] = jnp.sum(spread.T.reshape(LANES // traits, traits, traits), axis=0)


def finish(value_ref, form_ref, out_ref, score_ref, sems):
    first = pltpu.make_async_copy(value_ref, out_ref, sems.at[0])
    second = pltpu.make_async_copy(form_ref, score_ref, sems.at[1])
    first.start()
    second.start()
    first.wait()
    second.wait()


def shards(rows, cols, panel_t, kinship):
    traits, own = panel_t.shape
    plane = rows // cols * cols
    vmem = pltpu.VMEM
    dma = pltpu.SemaphoreType.DMA
    f32, bf16 = jnp.float32, jnp.bfloat16
    chunk = (traits // 2, 2 * own)
    value, score = (
        pl.pallas_call(
            functools.partial(kernel, rows, cols),
            out_shape=(vmem((traits, own), f32), vmem((traits, traits), f32)),
            in_specs=[pl.BlockSpec(memory_space=pl.ANY)] * 2,
            out_specs=(pl.BlockSpec(memory_space=vmem),) * 2,
            scratch_shapes=[
                vmem((traits, own), f32),
                vmem(chunk, f32),
                vmem(kinship.shape, f32),
                vmem(kinship.shape, bf16),
                vmem(kinship.shape, bf16),
                vmem(kinship.shape, bf16),
                vmem((cols,) + chunk, f32),
                vmem((plane,) + chunk, f32),
                vmem((cols,) + chunk, f32),
                vmem((cols,) + chunk, f32),
                vmem((rows * cols, traits * traits // LANES, LANES), f32),
            ]
            + [dma(())] * 10,
            compiler_params=pltpu.CompilerParams(collective_id=0, has_side_effects=True),
        )(panel_t, kinship)
    )
    return tuple(
        pl.pallas_call(
            finish,
            out_shape=(
                jax.ShapeDtypeStruct((traits, own), f32),
                jax.ShapeDtypeStruct((traits, traits), f32),
            ),
            in_specs=[pl.BlockSpec(memory_space=pl.ANY)] * 2,
            out_specs=(pl.BlockSpec(memory_space=pl.ANY),) * 2,
            scratch_shapes=[dma((2,))],
            compiler_params=pltpu.CompilerParams(vmem_limit_bytes=1024 * 1024),
        )(value, score)
    )


def solution(mesh):
    rows, cols = mesh.shape["rows"], mesh.shape["cols"]
    return jax.shard_map(
        functools.partial(shards, rows, cols),
        mesh=mesh,
        in_specs=(P(None, ("rows", "cols")), P("rows", "cols")),
        out_specs=(P(None, ("rows", "cols")), P()),
        check_vma=False,
    )
```

```python
import functools
import math

import jax
import jax.numpy as jnp
from jax import lax
from jax.experimental import pallas as pl
from jax.experimental.pallas import tpu as pltpu
from jax.sharding import PartitionSpec as P

MESH = pl.DeviceIdType.MESH
LANES = 128
SUBLANES = 8


def split(x):
    high = x.astype(jnp.bfloat16)
    rest = x - high.astype(jnp.float32)
    mid = rest.astype(jnp.bfloat16)
    low = (rest - mid.astype(jnp.float32)).astype(jnp.bfloat16)
    return high, mid, low


def dot(left, right, dims):
    n = left[0].shape[0]

    def one(pieces, weights):
        return lax.dot_general(
            jnp.concatenate(pieces, axis=0),
            weights,
            (dims, ((), ())),
            preferred_element_type=jnp.float32,
        )

    high, mid, low = one(left, right[0]), one(left[:2], right[1]), one(left[:1], right[2])
    small = high[2 * n :] + mid[n:] + low
    return high[:n] + (high[n : 2 * n] + mid[:n] + small)


def fold(x):
    half = x.shape[0] // 2
    return jnp.concatenate([x[:half], x[half:]], axis=1)


def unfold(x):
    own = x.shape[1] // 2
    return jnp.concatenate([x[:, :own], x[:, own:]], axis=0)


def join(chunks):
    own = chunks[0].shape[1] // 2
    return jnp.concatenate(
        [
            jnp.concatenate([x[:, :own] for x in chunks], axis=1),
            jnp.concatenate([x[:, own:] for x in chunks], axis=1),
        ],
        axis=0,
    )


def remote(src, dst, send, recv, where):
    return pltpu.make_async_remote_copy(
        src_ref=src,
        dst_ref=dst,
        send_sem=send,
        recv_sem=recv,
        device_id=where,
        device_id_type=MESH,
    )


def kernel(
    rows,
    cols,
    panel_hbm,
    kin_hbm,
    out_ref,
    score_ref,
    loaded,
    panel,
    kin,
    kin_high,
    kin_mid,
    kin_low,
    slab,
    block,
    part,
    landed,
    forms,
    panel_sem,
    kin_sem,
    slab_send,
    slab_recv,
    block_send,
    block_recv,
    part_send,
    part_recv,
    forms_send,
    forms_recv,
):
    count = rows * cols
    depth = rows // cols
    plane = depth * cols
    traits, own = panel_hbm.shape
    row, col = lax.axis_index("rows"), lax.axis_index("cols")
    me = row * cols + col
    zz = row // depth
    mine = me % plane

    def others(body):
        back = zz < cols // 2
        peers = [(col + step) % cols for step in range(cols)]

        def row_of(step, carry):
            r = jnp.where(back, row - step, row + step)
            r = jnp.where(r < 0, r + rows, jnp.where(r >= rows, r - rows, r))
            for c in peers:
                body((r, c))
            return carry

        lax.fori_loop(1, rows, row_of, 0, unroll=True)
        for c in peers[1:]:
            body((row, c))

    get_panel = pltpu.make_async_copy(panel_hbm, loaded, panel_sem)
    get_panel.start()
    barrier = pltpu.get_barrier_semaphore()
    others(
        lambda where: pl.semaphore_signal(
            barrier, inc=1, device_id=where, device_id_type=MESH
        )
    )
    get_kin = pltpu.make_async_copy(kin_hbm, kin, kin_sem)
    get_kin.start()
    get_panel.wait()
    panel[...] = fold(loaded[...])
    slab[col] = panel[...]
    pl.semaphore_wait(barrier, count - 1)

    for step in range(1, cols):
        c = (col + step) % cols
        remote(panel, slab.at[col], slab_send, slab_recv, (row, c)).start()

    keep_block = pltpu.make_async_copy(panel, block.at[mine], block_recv)
    send_block = remote(panel, block.at[mine], block_send, block_recv, (row, zz))
    sign = jnp.where(zz < cols // 2, rows - 1, 1)
    for step in range(1, rows):
        r = (row + sign * step) % rows
        remote(panel, block.at[mine], block_send, block_recv, (r, zz)).start()

    @pl.when(col == zz)
    def _():
        keep_block.start()

    @pl.when(col != zz)
    def _():
        send_block.start()

    def wait_bytes(ref, sem):
        pltpu.make_async_copy(ref, ref, sem).wait()

    get_kin.wait()
    kin_high[...], kin_mid[...], kin_low[...] = split(kin[...])
    wait_bytes(slab.at[pl.ds(0, cols - 1)], slab_recv)
    weights = (kin_high[...], kin_mid[...], kin_low[...])
    slab_panel = join([slab[c] for c in range(cols)])
    side = dot(split(slab_panel / math.sqrt(count * own)), weights, ((1,), (0,)))
    wide = tuple(jnp.concatenate([x] * (LANES // traits), axis=0) for x in split(side))

    wait_bytes(block, block_recv)
    block_panel = split(join([block[m] for m in range(plane)]))
    spread = dot(block_panel, wide, ((1,), (1,)))
    sublane = lax.broadcasted_iota(jnp.int32, (traits, LANES), 0) % SUBLANES
    group = lax.broadcasted_iota(jnp.int32, (traits, LANES), 1) // traits
    spread = jnp.where(sublane == group, spread, 0.0)
    forms[me] = jnp.sum(spread.reshape(traits // SUBLANES, SUBLANES, LANES), axis=1)
    others(
        lambda where: remote(
            forms.at[me], forms.at[me], forms_send, forms_recv, where
        ).start()
    )

    value = dot(block_panel, (kin_high[...], kin_mid[...], kin_low[...]), ((1,), (1,)))
    for c in range(cols):
        part[c] = fold(value[:, c * own : (c + 1) * own])
    for step in range(1, cols):
        c = (col + step) % cols
        remote(part.at[c], landed.at[col], part_send, part_recv, (row, c)).start()
    landed[col] = part[col]

    wait_bytes(landed.at[pl.ds(0, cols - 1)], part_recv)
    result = landed[0]
    for c in range(1, cols):
        result += landed[c]
    out_ref[...] = unfold(result)

    wait_bytes(block.at[pl.ds(0, rows - 1)], block_send)

    @pl.when(col != zz)
    def _():
        send_block.wait_send()

    wait_bytes(slab.at[pl.ds(0, cols - 1)], slab_send)
    wait_bytes(landed.at[pl.ds(0, cols - 1)], part_send)
    wait_bytes(forms.at[pl.ds(0, count - 1)], forms_send)
    wait_bytes(forms.at[pl.ds(0, count - 1)], forms_recv)
    total = jnp.sum(forms[...], axis=0)
    spread = jnp.concatenate(
        [
            jnp.broadcast_to(total[i : i + 1, :], (SUBLANES, LANES))
            for i in range(traits // SUBLANES)
        ],
        axis=0,
    )
    spread = jnp.where(sublane == group, spread, 0.0)
    score_ref[...] = jnp.sum(spread.T.reshape(LANES // traits, traits, traits), axis=0)


def finish(value_ref, form_ref, out_ref, score_ref, sems):
    first = pltpu.make_async_copy(value_ref, out_ref, sems.at[0])
    second = pltpu.make_async_copy(form_ref, score_ref, sems.at[1])
    first.start()
    second.start()
    first.wait()
    second.wait()


def shards(rows, cols, panel_t, kinship):
    traits, own = panel_t.shape
    plane = rows // cols * cols
    vmem = pltpu.VMEM
    dma = pltpu.SemaphoreType.DMA
    f32, bf16 = jnp.float32, jnp.bfloat16
    chunk = (traits // 2, 2 * own)
    value, score = (
        pl.pallas_call(
            functools.partial(kernel, rows, cols),
            out_shape=(vmem((traits, own), f32), vmem((traits, traits), f32)),
            in_specs=[pl.BlockSpec(memory_space=pl.ANY)] * 2,
            out_specs=(pl.BlockSpec(memory_space=vmem),) * 2,
            scratch_shapes=[
                vmem((traits, own), f32),
                vmem(chunk, f32),
                vmem(kinship.shape, f32),
                vmem(kinship.shape, bf16),
                vmem(kinship.shape, bf16),
                vmem(kinship.shape, bf16),
                vmem((cols,) + chunk, f32),
                vmem((plane,) + chunk, f32),
                vmem((cols,) + chunk, f32),
                vmem((cols,) + chunk, f32),
                vmem((rows * cols, traits * traits // LANES, LANES), f32),
            ]
            + [dma(())] * 10,
            compiler_params=pltpu.CompilerParams(collective_id=0, has_side_effects=True),
        )(panel_t, kinship)
    )
    return tuple(
        pl.pallas_call(
            finish,
            out_shape=(
                jax.ShapeDtypeStruct((traits, own), f32),
                jax.ShapeDtypeStruct((traits, traits), f32),
            ),
            in_specs=[pl.BlockSpec(memory_space=pl.ANY)] * 2,
            out_specs=(pl.BlockSpec(memory_space=pl.ANY),) * 2,
            scratch_shapes=[dma((2,))],
            compiler_params=pltpu.CompilerParams(vmem_limit_bytes=1024 * 1024),
        )(value, score)
    )


def solution(mesh):
    rows, cols = mesh.shape["rows"], mesh.shape["cols"]
    return jax.shard_map(
        functools.partial(shards, rows, cols),
        mesh=mesh,
        in_specs=(P(None, ("rows", "cols")), P("rows", "cols")),
        out_specs=(P(None, ("rows", "cols")), P()),
        check_vma=False,
    )
```
